32 devices in a mesh: passage: 4 (over z), cell: 4 (over y, x), tm: 2 (over core).
Axes of the slice: x: 2, y: 2, z: 4, core: 2. Of those that a mesh axis runs over, the one named last changes fastest.
Arguments:
- adjoint_start: float32 [8, 5, 8, 1024, 256], P('tm', None, 'cell', 'passage'), may hold values from -6 to 6
- adjoint_source: float32 [8, 5, 8, 1024, 256], P('tm', None, 'cell', 'passage'), may hold values from -6 to 6
- jacobian: bfloat16 [2, 5, 5, 8, 1024, 256], P(None, None, None, 'cell', 'passage'), may hold values from -2.5 to 2.5
- pseudo_time: float32 [8, 1024, 256], P('cell', 'passage'), may hold values from 3 to 12
- dissipation: float32 [8, 1024, 256], P('cell', 'passage'), may hold values from 0.2 to 1
- surface_cells: int32 [4, 1024], P('cell'), may hold values from 0 to 1023, as said below
- surface_weights: float32 [8, 5, 4096], P('tm', None, 'cell'), may hold values from -1 to 1
Outputs:
- adjoint_final: float32 [8, 5, 8, 1024, 256], P('tm', None, 'cell', 'passage')
- diameter_modes: float32 [2, 16, 4096], P(None, None, 'cell')
The draws below stay inside these ranges and needn't reach their ends.
Inputs may be any that keep to these rules, and one draw needn't show every extreme that they name: `surface_cells`: each row holds every value from 0 to 1023 exactly once, in a drawn order.
All inputs are finite; a program needn't handle non-finite values.
Results may differ from the reference program's by a relative error of at most 0.0025.
Values may be sent and summed in bfloat16 or wider, within the bound.
A program may use at most 256 MiB of HBM per device.

```python
import math
import jax
import jax.numpy as jnp
from jax import lax

NV = 5
NT = 8
PASSAGES = 16
CJ = 64
PITCH = 1024
CI = 2
CK = 256
SWEEPS = 2
NI = 8
SURF_DEV = 1024
SURF = 4096
N_CELL = 4


def draw_surface_cells(key, part):
    row_keys = jax.random.split(key, SURF // SURF_DEV)

    def one_block(row_key):
        return jax.random.permutation(row_key, SURF_DEV).astype(jnp.int32)
    return jax.vmap(one_block)(row_keys)


def level_of(stream_key, shape, shards, smallest, largest):
    level, own = 1.0, jax.random.fold_in(stream_key, 6)
    for axis_at, shards_of in shards:
        steps = jnp.exp(jax.random.uniform(jax.random.fold_in(own, axis_at), (shards_of,), jnp.float32, smallest / len(shards), largest / len(shards)))
        level = level * jnp.repeat(steps, shape[axis_at] // shards_of).reshape([-1 if axis == axis_at else 1 for axis in range(len(shape))])
    return level


def bell_draw(rng, extent, width, most, shards=(), kind=jnp.bfloat16):
    loudness = level_of(rng, extent, shards, -0.22, 0.18) if shards else 1.0
    entries = jax.random.normal(rng, extent, jnp.float32) * width * loudness
    return jnp.minimum(jnp.maximum(entries, -most), most).astype(kind)


def setup_inputs(seed: int = 0) -> dict:
    key_of = jax.random.split(jax.random.key(seed), 8)
    adjoint_start = bell_draw(key_of[0], (NT, NV, NI, PITCH, CK), 1.0, 6.0, ((0, 2), (2, 4), (3, 4)), jnp.float32)
    adjoint_source = bell_draw(key_of[1], (NT, NV, NI, PITCH, CK), 1.0, 6.0, ((0, 2), (2, 4), (3, 4)), jnp.float32)
    jacobian = bell_draw(key_of[2], (2, NV, NV, NI, PITCH, CK), NV ** -0.5, 2.5, ((3, 4), (4, 4)))
    pseudo_time = jnp.clip(jnp.exp(math.log(12.0) - 1.3862944 * jax.random.uniform(key_of[3], (NI, PITCH, CK), jnp.float32) ** level_of(key_of[3], (NI, PITCH, CK), ((0, 4), (1, 4)), -0.2, 0.2)), 3.0, 12.0)
    dissipation = jnp.clip(jnp.exp(math.log(1.0) - 1.609438 * jax.random.uniform(key_of[4], (NI, PITCH, CK), jnp.float32) ** level_of(key_of[4], (NI, PITCH, CK), ((0, 4), (1, 4)), -0.2, 0.2)), 0.2, 1.0)
    surface_cells = draw_surface_cells(jax.random.fold_in(key_of[7], 71), 0)
    surface_weights = bell_draw(key_of[6], (NT, NV, SURF), (NT * NV) ** -0.5, 1.0, ((0, 2), (2, 4)), jnp.float32)
    return dict(adjoint_start=adjoint_start, adjoint_source=adjoint_source, jacobian=jacobian, pseudo_time=pseudo_time, dissipation=dissipation, surface_cells=surface_cells, surface_weights=surface_weights)


OMEGA = 1.0


def spectral_matrix(total):
    index = jnp.arange(total, dtype=jnp.int32)
    offset = index[:, None] - index[None, :]
    parity = (1 - 2 * (offset % 2)).astype(jnp.float32)
    phase_arg = jnp.pi * offset.astype(jnp.float32) / total
    sine_safe = jnp.where(offset == 0, jnp.float32(1.0), jnp.sin(phase_arg))
    values = 0.5 * parity * jnp.cos(phase_arg) / sine_safe
    return jnp.where(offset == 0, jnp.float32(0.0), values)


def blade_table(passages):
    index = jnp.arange(passages, dtype=jnp.int32)
    product_mod = (index[:, None] * index[None, :]) % passages
    phase_arg = 2.0 * jnp.pi * product_mod.astype(jnp.float32) / passages
    factor = 1.0 / (passages ** 0.5)
    return jnp.stack([jnp.cos(phase_arg), -jnp.sin(phase_arg)]) * factor


def adjoint_operator(field, plus_i, minus_i, plus_j, minus_j, jacobian, sigma, damping):
    total_out = sigma * field + damping * (4.0 * field - plus_i - minus_i - plus_j - minus_j)
    variables = field.shape[1]
    flux_rows = []
    for target_var in range(variables):
        acc_flux = jnp.zeros_like(field[:, 0])
        for source_var in range(variables):
            acc_flux = acc_flux + jacobian[0, source_var, target_var].astype(jnp.float32) * (field[:, source_var] - plus_i[:, source_var])
            acc_flux = acc_flux + jacobian[1, source_var, target_var].astype(jnp.float32) * (field[:, source_var] - plus_j[:, source_var])
        flux_rows.append(acc_flux)
    return total_out + jnp.stack(flux_rows, axis=1)


def neighbours(field):
    zero_slab = jnp.zeros_like(field[:, :, :1])
    plus_i = jnp.concatenate([field[:, :, 1:], zero_slab], axis=2)
    minus_i = jnp.concatenate([zero_slab, field[:, :, :-1]], axis=2)
    plus_j = jnp.roll(field, -1, axis=3)
    minus_j = jnp.roll(field, 1, axis=3)
    return plus_i, minus_i, plus_j, minus_j


def reference(adjoint_start, adjoint_source, jacobian, pseudo_time, dissipation, surface_cells, surface_weights):
    start_rounded = adjoint_start.astype(jnp.bfloat16)
    dmatrix = spectral_matrix(NT)
    spectral_term = OMEGA * jnp.einsum('ab,avipk->bvipk', dmatrix, start_rounded.astype(jnp.float32), precision=lax.Precision.HIGHEST)
    scaling = 1.0 / (pseudo_time + 4.0 * dissipation)
    field = adjoint_start
    for sweep_index in range(SWEEPS):
        plus_i, minus_i, plus_j, minus_j = neighbours(field)
        applied = adjoint_operator(field, plus_i, minus_i, plus_j, minus_j, jacobian, pseudo_time, dissipation)
        field = field + (adjoint_source - applied - spectral_term) * scaling
    side_rows = (jnp.arange(PASSAGES, dtype=jnp.int32)[:, None] * CJ + jnp.arange(2, dtype=jnp.int32)[None, :] * (CJ - 1)).reshape(2 * PASSAGES)
    rows = jnp.take(field, side_rows, axis=3)
    rows = rows.reshape(NT, NV, N_CELL, CI, PASSAGES, 2, CK)
    rows = rows.transpose(0, 1, 4, 2, 5, 3, 6).reshape(NT, NV, PASSAGES, N_CELL * SURF_DEV)
    block_base = (jnp.arange(N_CELL, dtype=jnp.int32) * SURF_DEV)[:, None]
    global_index = (surface_cells + block_base).reshape(SURF).astype(jnp.int32)
    picked = jnp.take(rows, global_index, axis=3)
    sensitivity = jnp.einsum('tvs,tvps->ps', surface_weights, picked, precision=lax.Precision.HIGHEST)
    table = blade_table(PASSAGES)
    diameter_modes = jnp.einsum('cmp,ps->cms', table, sensitivity, precision=lax.Precision.HIGHEST)
    return field, diameter_modes
```

```python
import functools

import jax
import jax.numpy as jnp
from jax import lax
from jax.experimental import pallas as pl
from jax.experimental.pallas import tpu as pltpu
from jax.sharding import PartitionSpec as P

PASSAGES = 16
CJ = 64
SWEEPS = 2
OMEGA = 1.0
CHUNKS = 2
SUB = 16


def spectral_matrix(total):
    index = jnp.arange(total, dtype=jnp.int32)
    offset = index[:, None] - index[None, :]
    parity = (1 - 2 * (offset % 2)).astype(jnp.float32)
    phase_arg = jnp.pi * offset.astype(jnp.float32) / total
    sine_safe = jnp.where(offset == 0, jnp.float32(1.0), jnp.sin(phase_arg))
    values = 0.5 * parity * jnp.cos(phase_arg) / sine_safe
    return jnp.where(offset == 0, jnp.float32(0.0), values)


def blade_table(passages):
    index = jnp.arange(passages, dtype=jnp.int32)
    product_mod = index[:, None] * index[None, :] % passages
    phase_arg = 2.0 * jnp.pi * product_mod.astype(jnp.float32) / passages
    factor = 1.0 / passages**0.5
    return jnp.stack([jnp.cos(phase_arg), -jnp.sin(phase_arg)]) * factor


def rhs_kernel(odd_ref, own_ref, other_ref, field_ref, source_ref, *refs):
    *slabs, out_ref = refs
    chunks = len(slabs) // 2
    times, variables, cells, rows, _ = field_ref.shape
    per_chunk = times // chunks
    odd = odd_ref[0] == 1

    def one(step, carry):
        at = pl.ds(pl.multiple_of(step * SUB, SUB), SUB)
        for v in range(variables):
            theirs = []
            for a in range(times):
                c, t = divmod(a, per_chunk)
                pair = slabs[2 * c][t, v, at].astype(jnp.float32)
                diag = slabs[2 * c + 1][t, v, at].astype(jnp.float32)
                theirs.append((jnp.where(odd, pair, diag), jnp.where(odd, diag, pair)))
            for i in range(cells):
                mine = [
                    field_ref[a, v, i, at].astype(jnp.bfloat16).astype(jnp.float32)
                    for a in range(times)
                ]
                for b in range(times):
                    total = own_ref[0, b] * mine[0] + other_ref[0, b] * theirs[0][i]
                    for a in range(1, times):
                        total = total + own_ref[a, b] * mine[a]
                        total = total + other_ref[a, b] * theirs[a][i]
                    out_ref[b, v, i, at] = source_ref[b, v, i, at] - OMEGA * total
        return carry

    lax.fori_loop(0, rows // SUB, one, 0)


def sweep_kernel(last, blocks, odd_ref, field_ref, before_ref, after_ref, low_ref, high_ref, pair_ref,
                 diag_ref, rhs_ref, jac_ref, sigma_ref, damp_ref, *refs):
    if last:
        weights_ref, *rest = refs
        out_ref, sens_ref, step_i, step_j, part = rest[-5:]
    else:
        out_ref, pair_out, diag_out, step_i, step_j, part = refs
    times, variables, cells, rows, span = field_ref.shape
    block = pl.program_id(0)
    odd = odd_ref[0] == 1
    row = lax.broadcasted_iota(jnp.int32, (rows, span), 0)
    for i in range(cells):
        sigma = sigma_ref[i]
        damp = damp_ref[i]
        for t in range(times):
            for v in range(variables):
                f = field_ref[t, v, i]
                prev = before_ref[t, v, i, 7:8]
                prev = jnp.where(block == 0, low_ref[t, v, i : i + 1], prev)
                nxt = after_ref[t, v, i, 0:1]
                nxt = jnp.where(block == blocks - 1, high_ref[t, v, i : i + 1], nxt)
                plus_j = jnp.where(row == rows - 1, nxt, pltpu.roll(f, rows - 1, 0))
                minus_j = jnp.where(row == 0, prev, pltpu.roll(f, 1, 0))
                pair = pair_ref[t, v].astype(jnp.float32)
                diag = diag_ref[t, v].astype(jnp.float32)
                if i == cells - 1:
                    plus_i = jnp.where(odd, diag, pair)
                else:
                    plus_i = field_ref[t, v, i + 1]
                if i == 0:
                    minus_i = jnp.where(odd, pair, diag)
                else:
                    minus_i = field_ref[t, v, i - 1]
                step_i[t, v, i] = f - plus_i
                step_j[t, v, i] = f - plus_j
                part[t, v, i] = rhs_ref[t, v, i] - (
                    sigma * f + damp * (4.0 * f - plus_i - minus_i - plus_j - minus_j)
                )

    for i in range(cells):

        def one(step, carry):
            at = pl.ds(pl.multiple_of(step * SUB, SUB), SUB)
            scaling = 1.0 / (sigma_ref[i, at] + 4.0 * damp_ref[i, at])
            for v in range(variables):
                totals = [part[t, v, i, at] for t in range(times)]
                for u in range(variables):
                    along_i = jac_ref[0, u, v, i, at].astype(jnp.float32)
                    along_j = jac_ref[1, u, v, i, at].astype(jnp.float32)
                    for t in range(times):
                        totals[t] = totals[t] - along_i * step_i[t, u, i, at]
                        totals[t] = totals[t] - along_j * step_j[t, u, i, at]
                for t in range(times):
                    out_ref[t, v, i, at] = field_ref[t, v, i, at] + totals[t] * scaling
            return carry

        lax.fori_loop(0, rows // SUB, one, 0)

    if last:
        for side, at in ((0, 0), (1, rows - 1)):
            for i in range(cells):
                total = jnp.zeros((1, span), jnp.float32)
                for t in range(times):
                    for v in range(variables):
                        at_weight = side * cells + i
                        total = total + (
                            weights_ref[t, v, at_weight : at_weight + 1] * out_ref[t, v, i, at : at + 1]
                        )
                sens_ref[0, side * cells + i : side * cells + i + 1] = total
    else:
        for t in range(times):
            for v in range(variables):
                first = out_ref[t, v, 0]
                final = out_ref[t, v, cells - 1]
                pair_out[t, v] = jnp.where(odd, first, final).astype(jnp.bfloat16)
                diag_out[t, v] = jnp.where(odd, final, first).astype(jnp.bfloat16)


def smem():
    return pl.BlockSpec(memory_space=pltpu.SMEM)


def right_hand_side(odd, own, other, field, source, slabs):
    times, variables, cells, pitch, span = field.shape
    rows = min(2 * SUB, pitch)
    whole = pl.BlockSpec((times, variables, cells, rows, span), lambda j: (0, 0, 0, j, 0))
    slab = pl.BlockSpec((slabs[0].shape[0], variables, rows, span), lambda j: (0, 0, j, 0))
    size = field.size
    return pl.pallas_call(
        rhs_kernel,
        grid=(pitch // rows,),
        in_specs=[smem(), smem(), smem(), whole, whole] + [slab] * len(slabs),
        out_specs=whole,
        out_shape=jax.ShapeDtypeStruct(field.shape, jnp.float32),
        compiler_params=pltpu.CompilerParams(
            dimension_semantics=("arbitrary",), vmem_limit_bytes=48 << 20
        ),
        cost_estimate=pl.CostEstimate(flops=16 * size, bytes_accessed=14 * size, transcendentals=0),
        name="rhs",
    )(odd, own, other, field, source, *slabs)


def sweep(odd, field, at, low, high, pair, diag, rhs, jacobian, sigma, damp, chunk, weights=None, into=None):
    times, variables, span = pair.shape[0], pair.shape[1], pair.shape[3]
    cells, pitch = field.shape[2], field.shape[3]
    last = weights is not None
    rows = min(CJ, pitch)
    blocks, eighths = pitch // rows, rows // 8
    top = pitch // 8 - 1
    body = (times, variables, cells, rows, span)
    edge = (times, variables, cells, 8, span)
    in_specs = [
        smem(),
        pl.BlockSpec(body, lambda j: (at, 0, 0, j, 0)),
        pl.BlockSpec(edge, lambda j: (at, 0, 0, jnp.maximum(j * eighths - 1, 0), 0)),
        pl.BlockSpec(edge, lambda j: (at, 0, 0, jnp.minimum((j + 1) * eighths, top), 0)),
        pl.BlockSpec((times, variables, cells, span), lambda j: (0, 0, 0, 0)),
        pl.BlockSpec((times, variables, cells, span), lambda j: (0, 0, 0, 0)),
        pl.BlockSpec((times, variables, rows, span), lambda j: (0, 0, j, 0)),
        pl.BlockSpec((times, variables, rows, span), lambda j: (0, 0, j, 0)),
        pl.BlockSpec(body, lambda j: (chunk, 0, 0, j, 0)),
        pl.BlockSpec((2, variables, variables, cells, rows, span), lambda j: (0, 0, 0, 0, j, 0)),
        pl.BlockSpec((cells, rows, span), lambda j: (0, j, 0)),
        pl.BlockSpec((cells, rows, span), lambda j: (0, j, 0)),
    ]
    operands = [odd, field, field, field, low, high, pair, diag, rhs, jacobian, sigma, damp]
    aliases = {}
    if last:
        in_specs.append(
            pl.BlockSpec((times, variables, 2 * cells, span), lambda j: (chunk, 0, 0, 0))
        )
        operands.append(weights)
        if into is not None:
            in_specs.append(pl.BlockSpec(memory_space=pl.ANY))
            operands.append(into)
            aliases = {len(operands) - 1: 0}
        out_specs = [
            pl.BlockSpec(body, lambda j: (chunk, 0, 0, j, 0)),
            pl.BlockSpec((1, 2 * cells, span), lambda j: (j, 0, 0)),
        ]
        out_shape = [
            jax.ShapeDtypeStruct(rhs.shape, jnp.float32),
            jax.ShapeDtypeStruct((blocks, 2 * cells, span), jnp.float32),
        ]
    else:
        out_specs = [pl.BlockSpec(body, lambda j: (0, 0, 0, j, 0))] + [
            pl.BlockSpec((times, variables, rows, span), lambda j: (0, 0, j, 0))
        ] * 2
        out_shape = [jax.ShapeDtypeStruct((times, variables, cells, pitch, span), jnp.float32)] + [
            jax.ShapeDtypeStruct(pair.shape, jnp.bfloat16)
        ] * 2
    size = times * variables * cells * pitch * span
    return pl.pallas_call(
        functools.partial(sweep_kernel, last, blocks),
        grid=(blocks,),
        in_specs=in_specs,
        out_specs=out_specs,
        out_shape=out_shape,
        scratch_shapes=[pltpu.VMEM(body, jnp.float32)] * 3,
        input_output_aliases=aliases,
        compiler_params=pltpu.CompilerParams(
            dimension_semantics=("arbitrary",), vmem_limit_bytes=48 << 20
        ),
        cost_estimate=pl.CostEstimate(
            flops=40 * size, bytes_accessed=14 * size + 2 * jacobian.size, transcendentals=0
        ),
        name="sweep",
    )(*operands)


def body(
    relay,
    adjoint_start,
    adjoint_source,
    jacobian,
    pseudo_time,
    dissipation,
    surface_cells,
    surface_weights,
):
    times, variables, cells, pitch, span = adjoint_start.shape
    halves, columns, sectors = (lax.axis_size(name) for name in ("tm", "cell", "passage"))
    per_chunk = times // CHUNKS
    column = lax.axis_index("cell")
    half = lax.axis_index("tm")
    is_odd = column % 2 == 1
    odd = (column % 2).astype(jnp.int32).reshape(1)

    def pair_exchange(slab):
        perm = [(c, c ^ 1) for c in range(columns) if c ^ 1 < columns]
        return lax.ppermute(slab, "cell", perm)

    def diag_first(slab):
        hops = []
        for h in range(halves):
            one, two = (3, 0) if h == 0 else (0, 3)
            hops += [(1 * halves + h, one * halves + h), (2 * halves + h, two * halves + h)]
        return lax.ppermute(slab, ("cell", "tm"), hops)

    def diag_second(slab):
        hops = []
        for h in range(halves):
            one, two = (3, 0) if h == 0 else (0, 3)
            hops += [(one * halves + h, 2 * halves + h), (two * halves + h, 1 * halves + h)]
        return lax.ppermute(slab, ("cell", "tm"), hops)

    def diag_direct(slab):
        up = [(c, c + 1) for c in range(1, columns - 1, 2)]
        return lax.ppermute(slab, "cell", up + [(b, a) for a, b in up])

    def halos(pair, diag):
        if relay:
            diag = diag_first(diag)
            pair = pair_exchange(pair)
            return pair, diag_second(diag)
        return pair_exchange(pair), diag_direct(diag)

    def edges(field):
        up = [(i, (i + 1) % sectors) for i in range(sectors)]
        low = lax.ppermute(field[:, :, :, pitch - 1], "passage", up)
        high = lax.ppermute(field[:, :, :, 0], "passage", [(j, i) for i, j in up])
        return low, high

    dmatrix = spectral_matrix(times * halves)
    columns_own = lax.dynamic_slice_in_dim(dmatrix, half * times, times, 1)
    own = lax.dynamic_slice_in_dim(columns_own, half * times, times, 0)
    other = lax.dynamic_slice_in_dim(columns_own, (1 - half) * times, times, 0)

    swap = [(0, 1), (1, 0)]
    received, partner = [], []
    for c in range(CHUNKS):
        part = adjoint_start[c * per_chunk : (c + 1) * per_chunk]
        first, final = part[:, :, 0], part[:, :, cells - 1]
        pair = jnp.where(is_odd, first, final).astype(jnp.bfloat16)
        diag = jnp.where(is_odd, final, first).astype(jnp.bfloat16)
        received.append(halos(pair, diag))
        partner += [lax.ppermute(pair, "tm", swap), lax.ppermute(diag, "tm", swap)]
    low, high = edges(adjoint_start)
    rhs = right_hand_side(odd, own, other, adjoint_start, adjoint_source, partner)

    chosen = surface_cells[0]
    flat = jnp.arange(chosen.shape[0], dtype=jnp.int32)
    onehot = (chosen[:, None] == flat[None, :]).astype(jnp.float32)
    weights = jnp.einsum("tvs,se->tve", surface_weights, onehot, precision=lax.Precision.HIGHEST)
    weights = weights.reshape(times, variables, 2 * cells, span)

    fields = []
    for c in range(CHUNKS):
        pair, diag = received[c]
        part_low = low[c * per_chunk : (c + 1) * per_chunk]
        part_high = high[c * per_chunk : (c + 1) * per_chunk]
        field, pair, diag = sweep(
            odd, adjoint_start, c, part_low, part_high, pair, diag, rhs, jacobian, pseudo_time,
            dissipation, c,
        )
        fields.append((field, edges(field), halos(pair, diag)))

    final, sens = None, []
    for c in range(CHUNKS):
        field, (part_low, part_high), (pair, diag) = fields[c]
        final, part = sweep(
            odd, field, 0, part_low, part_high, pair, diag, rhs, jacobian, pseudo_time,
            dissipation, c, weights, final,
        )
        sens.append(part)

    total = functools.reduce(jnp.add, sens)
    blocks = total.shape[0]
    rows = pitch // blocks
    start = lax.axis_index("passage") * pitch + jnp.arange(blocks, dtype=jnp.int32) * rows
    owned = jnp.stack([start % CJ == 0, (start + rows) % CJ == 0], axis=1)
    total = total.reshape(blocks, 2, cells * span) * owned[:, :, None].astype(jnp.float32)
    total = total.reshape(blocks, 2 * cells * span)
    table = blade_table(PASSAGES)
    ours = (start[:, None] // CJ == jnp.arange(PASSAGES, dtype=jnp.int32)[None, :]).astype(jnp.float32)
    local_table = jnp.sum(table[:, :, None, :] * ours[None, None], axis=3)
    local = jnp.einsum("be,se->bs", total, onehot, precision=lax.Precision.HIGHEST)
    modes = jnp.sum(local_table[:, :, :, None] * local[None, None], axis=2)
    modes = modes + lax.ppermute(modes, "tm", swap)
    step = 1
    while step < sectors:
        modes = modes + lax.ppermute(modes, "passage", [(i, i ^ step) for i in range(sectors)])
        step *= 2
    return final, modes


def needs_relay(mesh):
    if mesh.shape["cell"] != 4:
        return False
    order = [mesh.axis_names.index(name) for name in ("cell", "passage", "tm")]
    grid = mesh.devices.transpose(order)
    at = [getattr(grid[c, 0, 0], "coords", None) for c in range(4)]
    if any(a is None for a in at):
        return False
    apart = lambda a, b: sum(abs(p - q) for p, q in zip(at[a], at[b]))
    return apart(1, 2) == 2 and all(apart(a, b) == 1 for a, b in ((0, 1), (2, 3), (0, 2), (1, 3)))


def solution(mesh):
    in_specs = (
        P("tm", None, "cell", "passage", None),
        P("tm", None, "cell", "passage", None),
        P(None, None, None, "cell", "passage", None),
        P("cell", "passage", None),
        P("cell", "passage", None),
        P("cell", None),
        P("tm", None, "cell"),
    )
    out_specs = (P("tm", None, "cell", "passage", None), P(None, None, "cell"))
    return jax.shard_map(
        functools.partial(body, needs_relay(mesh)),
        mesh=mesh,
        in_specs=in_specs,
        out_specs=out_specs,
        check_vma=False,
    )
```
